128 devices in a mesh: expert: 64 (over z, y, x), pair: 2 (over core).
Axes of the slice: x: 4, y: 4, z: 4, core: 2. Of those that a mesh axis runs over, the one named last changes fastest.
Arguments:
- tokens: bfloat16 [16384, 2048], P(('expert', 'pair')), may hold values from -6 to 6
- out_grads: bfloat16 [16384, 2048], P(('expert', 'pair')), may hold values from -60 to 60
- routing: int32 [16384, 8], P(('expert', 'pair')), may hold values from 0 to 63, all different within a row; in each aligned block of 128 rows (0 to 127, 128 to 255, ...) at most 21 rows name the same one
- combine: float32 [16384, 8], P(('expert', 'pair')), may hold values from 0.05 to 0.3
- weights: bfloat16 [2, 64, 768, 2048], P('pair', 'expert'), may hold values from -6 to 6
- momentum: float32 [2, 64, 768, 2048], P('pair', 'expert'), may hold values from -40 to 40
Outputs:
- momentum_out: float32 [2, 64, 768, 2048], P('pair', 'expert')
- rollout_weights: bfloat16 [2, 64, 768, 2048], P(None, 'expert', 'pair')
The draws below stay inside these ranges and needn't reach their ends.
Inputs may be any that keep to these rules, and one draw needn't show every extreme that they name: `routing`: each row names 8 different experts; within the 128 rows of one device no expert is named more than 21 times, and in some device's rows some expert is named exactly 21 times.
All inputs are finite; a program needn't handle non-finite values.
Results may differ from the reference program's by a relative error of at most 0.005.
Values may be sent and summed in bfloat16 or wider, within the bound.
No kernel may reach another device: no remote copies, remote signals or barrier semaphores. Data moves between devices by JAX's collectives and lax.ppermute only.
A program may use at most 128 MiB of HBM per device.

```python
import math
import jax
import jax.numpy as jnp
import numpy as np
from jax import lax

D = 2048
FF = 768
TOPK = 8
TOK_DEV = 128
NS_ITERS = 2
EXPERTS = 64
TOKENS = 16384
CAP = 21
N_EXPERT = 64
N_PAIR = 2


def draw_momentum(key, part):
    key_entries = jax.random.fold_in(key, 11)
    key_rows = jax.random.fold_in(key, 12)
    key_columns = jax.random.fold_in(key, 13)
    row_scale = jnp.exp(jax.random.uniform(key_rows, (2, EXPERTS, FF, 1), jnp.float32, -1.15, 1.15))
    column_scale = jnp.exp(jax.random.uniform(key_columns, (2, EXPERTS, 1, D), jnp.float32, -1.15, 1.15))
    entries = jax.random.normal(key_entries, (2, EXPERTS, FF, D), jnp.float32)
    return jnp.clip(entries * row_scale * column_scale, -40.0, 40.0).astype(jnp.float32)


def level_of(key, extent, split, smallest, largest):
    level = 1.0
    for dim, shards_of in split:
        draws = jax.random.uniform(jax.random.fold_in(jax.random.fold_in(key, 6), dim), (shards_of,), jnp.float32, smallest / len(split), largest / len(split))
        level = level * jnp.repeat(jnp.exp(draws), extent[dim] // shards_of).reshape((-1,) + (1,) * (len(extent) - 1 - dim))
    return level


def shared_out(stream_key, own, number, rows, amount, top, reach, lean):
    order = jax.random.permutation(stream_key, amount)
    crowded, ordinary = shares(amount, rows * top, reach, lean, True), shares(amount, rows * top, reach, lean, False)
    places = jnp.arange(amount)

    def named(lengths, turn):
        used = int((lengths > 0).sum())
        fixed = max(1, used // 4)
        passed = fixed + (places - fixed + turn * (used - fixed)) % max(1, amount - fixed)
        return jnp.zeros((amount,), jnp.int32).at[order[jnp.where(places < fixed, places, passed)]].set(jnp.asarray(lengths, jnp.int32))

    lengths = jnp.where(number % 4 == 0, named(crowded, number // 4), named(ordinary, number - number // 4 - 1))
    mixed = jax.random.permutation(jax.random.fold_in(own, 3), amount)
    source_of, taker = mixed[0:amount // 2 * 2:2], mixed[1:amount // 2 * 2:2]
    slack = jnp.minimum(lengths[source_of] - 1, reach - lengths[taker]) // 2
    slack = jnp.where((source_of == order[0]) | (taker == order[0]) | (lengths[taker] == 0), 0, jnp.maximum(slack, 0))
    passed = jax.random.randint(jax.random.fold_in(own, 4), (amount // 2,), 0, 1 << 20) % (slack + 1)
    lengths = lengths.at[source_of].add(-passed).at[taker].add(passed)
    labels = jnp.searchsorted(jnp.cumsum(lengths), jnp.arange(rows * top), side="right").astype(jnp.int32)
    grid = labels.reshape(top, rows).T
    grid = grid[jax.random.permutation(jax.random.fold_in(own, 1), rows)]
    turn = jax.random.randint(jax.random.fold_in(own, 2), (rows, 1), 0, top)
    return jnp.take_along_axis(grid, (jnp.arange(top)[None, :] + turn) % top, axis=1)


def shares(number_of, total, limit, skew, full):
    portions = [(1 << 20) // math.isqrt(rank ** skew) + 1 for rank in range(1, number_of + 1)]
    largest = limit if full else min(limit, max(-(-total // number_of), total * portions[0] // sum(portions)))
    least = 1 if total - largest >= number_of - 1 else 0
    holding, surplus = [largest] + [least] * (number_of - 1), total - largest - least * (number_of - 1)
    while surplus > 0:
        free = [i for i in range(1, number_of) if holding[i] < largest] or [i for i in range(1, number_of) if holding[i] < limit]
        whole, left = sum([portions[i] for i in free]), surplus
        for i in free:
            extra = min(limit - holding[i], max(1, left * portions[i] // whole), surplus)
            holding[i] = holding[i] + extra
            surplus = surplus - extra
    return np.array(holding)


def gaussian(stream_key, dims, scale, bound, split=(), kind=jnp.bfloat16):
    loudness = level_of(stream_key, dims, split, -0.22, 0.18) if split else 1.0
    drawn = jax.random.normal(stream_key, dims, jnp.float32) * scale * loudness
    return jnp.minimum(jnp.maximum(drawn, -bound), bound).astype(kind)


def setup_inputs(seed: int = 0) -> dict:
    key_list = jax.random.split(jax.random.key(seed), 7)
    tokens = gaussian(key_list[0], (TOKENS, D), 1.0, 6.0, ((0, 128),))
    out_grads = gaussian(key_list[1], (TOKENS, D), 10.0, 60.0, ((0, 128),))
    routing_keys = jax.random.split(jax.random.fold_in(key_list[2], 1), TOKENS // TOK_DEV)
    routing_turns = jax.random.permutation(jax.random.fold_in(key_list[2], 3), TOKENS // TOK_DEV)
    routing = jax.vmap(lambda own, number: shared_out(jax.random.fold_in(key_list[2], 2), own, number, TOK_DEV, EXPERTS, TOPK, CAP, 2))(routing_keys, routing_turns).reshape((TOKENS, TOPK))
    combine = jnp.clip(0.05 + 0.25 * jax.random.uniform(key_list[3], (TOKENS, TOPK), jnp.float32) ** level_of(key_list[3], (TOKENS, TOPK), ((0, 128),), -0.2, 0.2), 0.05, 0.3)
    weights = gaussian(key_list[4], (2, EXPERTS, FF, D), 1.0, 6.0, ((0, 2), (1, 64)))
    momentum = draw_momentum(jax.random.fold_in(key_list[6], 71), 0)
    return dict(tokens=tokens, out_grads=out_grads, routing=routing, combine=combine, weights=weights, momentum=momentum)


COEF_A = 3.4445
COEF_B = -4.775
COEF_C = 2.0315
DECAY = 0.9
NORM_EPS = 1e-07

def product(left_side, right_side):
    return jnp.dot(left_side.astype(jnp.float32), right_side.astype(jnp.float32), precision=lax.Precision.HIGHEST, preferred_element_type=jnp.float32)

def newton_schulz(matrix):
    frobenius = jnp.sqrt(jnp.sum(matrix * matrix))
    orthogonal = (matrix / (frobenius + NORM_EPS)).astype(jnp.bfloat16)
    for iteration in range(NS_ITERS):
        gram_matrix = product(orthogonal, orthogonal.T).astype(jnp.bfloat16)
        polynomial = (COEF_B * gram_matrix.astype(jnp.float32) + COEF_C * product(gram_matrix, gram_matrix)).astype(jnp.bfloat16)
        orthogonal = (COEF_A * orthogonal.astype(jnp.float32) + product(polynomial, orthogonal)).astype(jnp.bfloat16)
    return orthogonal

def reference(tokens, out_grads, routing, combine, weights, momentum):
    flat_expert = routing.reshape(-1).astype(jnp.int32)
    flat_weight = combine.reshape(-1)
    total = flat_expert.shape[0]
    flat_token = (jnp.arange(total, dtype=jnp.int32) // TOPK).astype(jnp.int32)
    most_rows = N_EXPERT * N_PAIR * CAP
    inv_width = 1.0 / math.sqrt(D)
    inv_hidden = 1.0 / math.sqrt(FF)
    step_size = 0.5 * math.sqrt(D)

    def per_expert(expert):
        elsewhere = (flat_expert != expert).astype(jnp.int32)
        ranking = jnp.argsort(elsewhere * total + jnp.arange(total, dtype=jnp.int32))[:most_rows].astype(jnp.int32)
        matched = elsewhere[ranking] == 0
        picked = flat_token[ranking]
        x_rows = jnp.where(matched[:, None], tokens[picked], 0).astype(jnp.bfloat16)
        scaled = out_grads[picked].astype(jnp.float32) * flat_weight[ranking][:, None]
        scaled_rows = jnp.where(matched[:, None], scaled, 0.0).astype(jnp.bfloat16)
        up_weight = weights[0, expert]
        down_weight = weights[1, expert]
        pre_act = product(x_rows, up_weight.T) * inv_width
        squash = jax.nn.sigmoid(pre_act)
        hidden = (pre_act * squash).astype(jnp.bfloat16)
        hidden_grad = product(scaled_rows, down_weight.T) * inv_hidden
        pre_grad = (hidden_grad * squash * (1.0 + pre_act * (1.0 - squash))).astype(jnp.bfloat16)
        grad_up = product(pre_grad.T, x_rows) * inv_width
        grad_down = product(hidden.T, scaled_rows) * inv_hidden
        velocity_up = DECAY * momentum[0, expert] + grad_up
        velocity_down = DECAY * momentum[1, expert] + grad_down
        new_up = (up_weight.astype(jnp.float32) - step_size * newton_schulz(velocity_up).astype(jnp.float32)).astype(jnp.bfloat16)
        new_down = (down_weight.astype(jnp.float32) - step_size * newton_schulz(velocity_down).astype(jnp.float32)).astype(jnp.bfloat16)
        return (jnp.stack([velocity_up, velocity_down]), jnp.stack([new_up, new_down]))
    velocities, updated = lax.map(per_expert, jnp.arange(EXPERTS, dtype=jnp.int32))
    return (jnp.swapaxes(velocities, 0, 1), jnp.swapaxes(updated, 0, 1))
```

```python
import math

import jax
import jax.numpy as jnp
from jax import lax
from jax.experimental import pallas as pl
from jax.experimental.pallas import tpu as pltpu
from jax.sharding import PartitionSpec as P

D = 2048
FF = 768
TOK = 128
CAP = 21
N_CHIP = 64
ROWS = 2 * CAP
BLOCK = ROWS * D // 128
MAIN = 40 * N_CHIP
REST = 2 * N_CHIP
NS_ITERS = 2

COEF_A = 3.4445
COEF_B = -4.775
COEF_C = 2.0315
DECAY = 0.9
NORM_EPS = 1e-07
STEP = 0.5 * math.sqrt(D)
BF16 = jnp.bfloat16
F32 = jnp.float32
SWAP = [(0, 1), (1, 0)]


def nt_dot(left, right):
    return lax.dot_general(left, right, (((1,), (1,)), ((), ())), preferred_element_type=F32)


def nn_dot(left, right):
    return lax.dot_general(left, right, (((1,), (0,)), ((), ())), preferred_element_type=F32)


def dispatch_kernel(core_ref, keep_ref, got_ref, own_tab, got_tab, out_ref, data, table, slots, rest):
    step = pl.program_id(0)
    first = core_ref[0] == 0

    @pl.when(step == 0)
    def _():
        keep, got = keep_ref[...], got_ref[...]
        data[0:TOK, :] = jnp.where(first, keep, got)
        data[TOK : 2 * TOK, :] = jnp.where(first, got, keep)
        own, other = own_tab[...], got_tab[...]
        before = (
            lax.broadcasted_iota(jnp.int32, (TOK, TOK), 0)
            < lax.broadcasted_iota(jnp.int32, (TOK, TOK), 1)
        ).astype(F32).astype(BF16)
        for half, part in enumerate((jnp.where(first, own, other), jnp.where(first, other, own))):
            routed = part > 0.0
            earlier = nn_dot(jnp.where(routed, 1.0, 0.0).astype(BF16), before)
            columns = slice(half * TOK, (half + 1) * TOK)
            table[:, columns] = part
            slots[:, columns] = jnp.where(routed, earlier + float(half * CAP), -1.0)

    row_id = lax.broadcasted_iota(jnp.int32, (48, 2 * TOK), 0).astype(F32)
    picks, scales = [], []
    for e in range(8):
        slot_row = slots[pl.ds(step * 8 + e, 1), :]
        weight_row = table[pl.ds(step * 8 + e, 1), :]
        hit = row_id == slot_row
        picks.append(jnp.where(hit, 1.0, 0.0).astype(BF16))
        weight = jnp.sum(jnp.where(hit, weight_row, 0.0), axis=1, keepdims=True)
        scales.append(jnp.where(first, 1.0, weight))
    pick = jnp.concatenate(picks, axis=0)
    for c in range(8):
        value = nn_dot(pick, data[:, c * 256 : (c + 1) * 256])
        for e in range(8):
            piece = value[e * 48 : (e + 1) * 48, :] * scales[e]
            for h in range(2):
                j = 2 * c + h
                part = piece[:, h * 128 : (h + 1) * 128]
                out_ref[e, j * 16 : j * 16 + 16, :] = part[0:16].astype(BF16)
                out_ref[e, 256 + j * 16 : 256 + j * 16 + 16, :] = part[16:32].astype(BF16)
                for r in range(2):
                    at = (e * 2 + r) * 16 + j
                    rest[at : at + 1, :] = part[40 + r : 41 + r]
            mixed = jnp.concatenate([piece[32:40, 0:128], piece[32:40, 128:256]], axis=0)
            out_ref[e, 512 + c * 16 : 512 + c * 16 + 16, :] = mixed.astype(BF16)
    for e in range(8):
        for r in range(2):
            at = (e * 2 + r) * 16
            out_ref[e, 640 + r * 16 : 656 + r * 16, :] = rest[at : at + 16, :].astype(BF16)


def dispatch(core, keep, got, own_tab, got_tab):
    whole = lambda *shape: pl.BlockSpec(shape, lambda i: (0,) * len(shape))
    return pl.pallas_call(
        dispatch_kernel,
        out_shape=jax.ShapeDtypeStruct((N_CHIP, BLOCK, 128), BF16),
        grid=(8,),
        in_specs=[
            pl.BlockSpec(memory_space=pltpu.SMEM),
            whole(TOK, D),
            whole(TOK, D),
            whole(N_CHIP, TOK),
            whole(N_CHIP, TOK),
        ],
        out_specs=pl.BlockSpec((8, BLOCK, 128), lambda i: (i, 0, 0)),
        scratch_shapes=[
            pltpu.VMEM((2 * TOK, D), BF16),
            pltpu.VMEM((N_CHIP, 2 * TOK), F32),
            pltpu.VMEM((N_CHIP, 2 * TOK), F32),
            pltpu.VMEM((256, 128), F32),
        ],
        cost_estimate=pl.CostEstimate(flops=3_200_000_000, bytes_accessed=13_000_000, transcendentals=0),
        name="dispatch",
    )(core, keep, got, own_tab, got_tab)


def project_kernel(core_ref, recv_ref, weight_ref, rows_ref, rest_ref, factor_ref, give_ref, rest_factor_ref, rest_give_ref, rest):
    step = pl.program_id(0)
    first = core_ref[0] == 0
    scale = jnp.where(first, 1.0 / math.sqrt(D), 1.0 / math.sqrt(FF))
    for pair in range(8):
        base = pair * 80
        for j in range(16):
            columns = slice(j * 128, (j + 1) * 128)
            for s in range(2):
                for b in range(2):
                    at = base + (2 * s + b) * 16
                    rows_ref[at : at + 16, columns] = recv_ref[2 * pair + s, b * 256 + j * 16 : b * 256 + j * 16 + 16, :]
        for c in range(8):
            top = recv_ref[2 * pair, 512 + c * 16 : 528 + c * 16, :].astype(F32)
            low = recv_ref[2 * pair + 1, 512 + c * 16 : 528 + c * 16, :].astype(F32)
            for h in range(2):
                mixed = jnp.concatenate([top[8 * h : 8 * h + 8], low[8 * h : 8 * h + 8]], axis=0)
                rows_ref[base + 64 : base + 80, (2 * c + h) * 128 : (2 * c + h + 1) * 128] = mixed.astype(BF16)
    for s in range(16):
        for r in range(2):
            at = (2 * s + r) * 16
            rest[at : at + 16, :] = recv_ref[s, 640 + r * 16 : 656 + r * 16, :].astype(F32)
    rest_at = pl.ds(pl.multiple_of(step * 32, 32), 32)
    for j in range(16):
        rest_ref[rest_at, j * 128 : (j + 1) * 128] = rest[pl.ds(j, 32, stride=16), :].astype(BF16)

    def finish(product, factor_out, give_out, block):
        pre = product * scale
        squash = 1.0 / (1.0 + jnp.exp(-pre))
        factor_out[block, :] = jnp.where(first, squash * (1.0 + pre * (1.0 - squash)), 1.0)
        give_out[block, :] = jnp.where(first, pre * squash, pre).astype(BF16)

    for m in range(3):
        block = slice(m * 256, (m + 1) * 256)
        finish(nt_dot(weight_ref[block, :], rows_ref[...]), factor_ref, give_ref, block)

    @pl.when(step == 3)
    def _():
        for m in range(3):
            block = slice(m * 256, (m + 1) * 256)
            finish(nt_dot(weight_ref[block, :], rest_ref[...]), rest_factor_ref, rest_give_ref, block)


def project(core, recv, weight):
    whole = lambda *shape: pl.BlockSpec(shape, lambda i: (0,) * len(shape))
    return pl.pallas_call(
        project_kernel,
        out_shape=(
            jax.ShapeDtypeStruct((MAIN, D), BF16),
            jax.ShapeDtypeStruct((REST, D), BF16),
            jax.ShapeDtypeStruct((FF, MAIN), F32),
            jax.ShapeDtypeStruct((FF, MAIN), BF16),
            jax.ShapeDtypeStruct((FF, REST), F32),
            jax.ShapeDtypeStruct((FF, REST), BF16),
        ),
        grid=(4,),
        in_specs=[
            pl.BlockSpec(memory_space=pltpu.SMEM),
            pl.BlockSpec((16, BLOCK, 128), lambda i: (i, 0, 0)),
            whole(FF, D),
        ],
        out_specs=(
            pl.BlockSpec((640, D), lambda i: (i, 0)),
            whole(REST, D),
            pl.BlockSpec((FF, 640), lambda i: (0, i)),
            pl.BlockSpec((FF, 640), lambda i: (0, i)),
            whole(FF, REST),
            whole(FF, REST),
        ),
        scratch_shapes=[pltpu.VMEM((512, 128), F32)],
        cost_estimate=pl.CostEstimate(flops=8_500_000_000, bytes_accessed=38_000_000, transcendentals=2_000_000),
        compiler_params=pltpu.CompilerParams(vmem_limit_bytes=60 * 1024 * 1024),
        name="project",
    )(core, recv, weight)


def update_kernel(
    core_ref, rows_ref, factor_ref, back_ref, rest_ref, rest_factor_ref, rest_back_ref, weight_hbm, momentum_hbm,
    velocity_hbm, new_ref, total, held, weight, ortho, gram, poly, sems,
):
    step = pl.program_id(0)
    first = core_ref[0] == 0
    scale = jnp.where(first, 1.0 / math.sqrt(D), 1.0 / math.sqrt(FF))
    momentum_in = pltpu.make_async_copy(momentum_hbm, held, sems.at[0])
    weight_in = pltpu.make_async_copy(weight_hbm, weight, sems.at[1])
    velocity_out = pltpu.make_async_copy(held, velocity_hbm, sems.at[2])

    @pl.when(step == 0)
    def _():
        momentum_in.start()
        weight_in.start()
        for m in range(3):
            block = slice(m * 256, (m + 1) * 256)
            side = (rest_back_ref[block, :].astype(F32) * rest_factor_ref[block, :]).astype(BF16)
            total[block, :] = nn_dot(side, rest_ref[...])

    for m in range(3):
        block = slice(m * 256, (m + 1) * 256)
        side = (back_ref[block, :].astype(F32) * factor_ref[block, :]).astype(BF16)
        for c in range(4):
            columns = slice(c * 512, (c + 1) * 512)
            total[block, columns] += nn_dot(side, rows_ref[:, columns])

    @pl.when(step == 3)
    def _():
        momentum_in.wait()
        squares = jnp.zeros((8, D), F32)
        for m in range(12):
            block = slice(m * 64, (m + 1) * 64)
            velocity = DECAY * held[block, :] + total[block, :] * scale
            held[block, :] = velocity
            square = velocity * velocity
            for k in range(8):
                squares = squares + square[k * 8 : (k + 1) * 8, :]
        velocity_out.start()
        inverse = 1.0 / (jnp.sqrt(jnp.sum(squares)) + NORM_EPS)
        for m in range(12):
            block = slice(m * 64, (m + 1) * 64)
            ortho[block, :] = (held[block, :] * inverse).astype(BF16)
        for iteration in range(NS_ITERS):
            for m in range(3):
                block = slice(m * 256, (m + 1) * 256)
                gram[block, :] = nt_dot(ortho[block, :], ortho[...]).astype(BF16)
            for m in range(3):
                block = slice(m * 256, (m + 1) * 256)
                square = nn_dot(gram[block, :], gram[...])
                poly[block, :] = (COEF_B * gram[block, :].astype(F32) + COEF_C * square).astype(BF16)
            if iteration == NS_ITERS - 1:
                weight_in.wait()
            for c in range(8):
                columns = slice(c * 256, (c + 1) * 256)
                product = nn_dot(poly[...], ortho[:, columns])
                fresh = (COEF_A * ortho[:, columns].astype(F32) + product).astype(BF16)
                if iteration < NS_ITERS - 1:
                    ortho[:, columns] = fresh
                else:
                    for half in range(2):
                        part = slice(half * 384, (half + 1) * 384)
                        new_ref[half, :, columns] = (
                            weight[part, columns].astype(F32) - STEP * fresh[part, :].astype(F32)
                        ).astype(BF16)
        velocity_out.wait()


def update(core, rows, factor, back, rest, rest_factor, rest_back, weight, momentum):
    whole = lambda *shape: pl.BlockSpec(shape, lambda i: (0,) * len(shape))
    anywhere = pl.BlockSpec(memory_space=pl.ANY)
    return pl.pallas_call(
        update_kernel,
        out_shape=(
            jax.ShapeDtypeStruct((FF, D), F32),
            jax.ShapeDtypeStruct((2, FF // 2, D), BF16),
        ),
        grid=(4,),
        in_specs=[
            pl.BlockSpec(memory_space=pltpu.SMEM),
            pl.BlockSpec((640, D), lambda i: (i, 0)),
            pl.BlockSpec((FF, 640), lambda i: (0, i)),
            pl.BlockSpec((FF, 640), lambda i: (0, i)),
            whole(REST, D),
            whole(FF, REST),
            whole(FF, REST),
            anywhere,
            anywhere,
        ],
        out_specs=(anywhere, whole(2, FF // 2, D)),
        scratch_shapes=[
            pltpu.VMEM((FF, D), F32),
            pltpu.VMEM((FF, D), F32),
            pltpu.VMEM((FF, D), BF16),
            pltpu.VMEM((FF, D), BF16),
            pltpu.VMEM((FF, FF), BF16),
            pltpu.VMEM((FF, FF), BF16),
            pltpu.SemaphoreType.DMA((3,)),
        ],
        cost_estimate=pl.CostEstimate(flops=20_000_000_000, bytes_accessed=45_000_000, transcendentals=0),
        compiler_params=pltpu.CompilerParams(vmem_limit_bytes=60 * 1024 * 1024),
        name="update",
    )(core, rows, factor, back, rest, rest_factor, rest_back, weight, momentum)


def on_device(tokens, out_grads, routing, combine, weights, momentum):
    core = lax.axis_index("pair").astype(jnp.int32)
    first = core == 0
    chosen = routing.T[:, None, :] == jnp.arange(N_CHIP, dtype=jnp.int32)[None, :, None]
    own_tab = jnp.sum(jnp.where(chosen, combine.T[:, None, :], 0.0), axis=0)
    got_tab = lax.ppermute(own_tab, "pair", SWAP)
    keep = jnp.where(first, tokens, out_grads)
    got = lax.ppermute(jnp.where(first, out_grads, tokens), "pair", SWAP)
    which = core.reshape(1)
    send = dispatch(which, keep, got, own_tab, got_tab)
    recv = lax.all_to_all(send, "expert", split_axis=0, concat_axis=0, tiled=True)
    weight = weights[0, 0]
    rows, rest, factor, give, rest_factor, rest_give = project(which, recv, weight)
    back = lax.ppermute(give, "pair", SWAP)
    rest_back = lax.ppermute(rest_give, "pair", SWAP)
    velocity, fresh = update(which, rows, factor, back, rest, rest_factor, rest_back, weight, momentum[0, 0])
    rollout = lax.all_to_all(fresh, "pair", split_axis=0, concat_axis=0, tiled=True)
    return (velocity[None, None], rollout[:, None])


def solution(mesh):
    return jax.shard_map(
        on_device,
        mesh=mesh,
        in_specs=(
            P(("expert", "pair"), None),
            P(("expert", "pair"), None),
            P(("expert", "pair"), None),
            P(("expert", "pair"), None),
            P("pair", "expert", None, None),
            P("pair", "expert", None, None),
        ),
        out_specs=(P("pair", "expert", None, None), P(None, "expert", "pair", None)),
        check_vma=False,
    )
```
